128 devices in a mesh: ctx: 32 (over x_hi, z, y), tp: 4 (over x_lo, core).
Axes of the slice: x: 4 (x_hi: 2, x_lo: 2; x = x_hi * 2 + x_lo), y: 4, z: 4, core: 2. Of those that a mesh axis runs over, the one named last changes fastest.
Arguments:
- tokens: bfloat16 [16384, 6144], P(('ctx', 'tp')), may hold values from -18 to 18
- w_query: bfloat16 [6144, 3072], P(None, 'tp'), may hold values from -1 to 1
- key_matrix: bfloat16 [6144, 512], P(None, 'tp'), may hold values from -1 to 1
- value_matrix: bfloat16 [6144, 512], P(None, 'tp'), may hold values from -0.078125 to 0.078125
- w_out: bfloat16 [3072, 6144], P('tp'), may hold values from -0.109375 to 0.109375
- span_order: int32 [32, 2], replicated, may hold values from 0 to 63, as said below
Outputs:
- attended: bfloat16 [16384, 6144], P(('ctx', 'tp'))
The draws below stay inside these ranges and needn't reach their ends.
Inputs may be any that keep to these rules, and one draw needn't show every extreme that they name: `span_order`: row r is (p, 63 - p) with p a permutation of 0 to 31, so every span appears once.
All inputs are finite; a program needn't handle non-finite values.
Results may differ from the reference program's by a relative error of at most 0.014.
The reference program's roundings to bfloat16 on the way count: a program that leaves them out, or rounds other values in their place, can miss the bound.
Values may be sent and summed in bfloat16 or wider, within the bound.
No kernel may reach another device: no remote copies, remote signals or barrier semaphores. Data moves between devices by JAX's collectives and lax.ppermute only.
A program may use at most 128 MiB of HBM per device.

```python
import math
import jax
import jax.numpy as jnp
from jax import lax

MODEL_WIDTH = 6144
QUERY_HEADS = 24
KEY_HEADS = 4
HEAD_SIZE = 128
SPAN_TOKENS = 256
QUERY_PER_KEY = 6
SEQUENCE_TOKENS = 16384
N_CTX = 32
N_TP = 4


def unrotated_query(key):
    return jax.random.normal(jax.random.fold_in(key, 11), (MODEL_WIDTH, QUERY_HEADS * HEAD_SIZE), jnp.float32) * (3.0 / math.sqrt(MODEL_WIDTH))


def draw_w_query(key, part):
    return jnp.clip(unrotated_query(key), -1.0, 1.0).astype(jnp.bfloat16)


def draw_key_matrix(key, part):
    random_noise = jax.random.normal(jax.random.fold_in(key, 23), (MODEL_WIDTH, KEY_HEADS * HEAD_SIZE), jnp.float32) / math.sqrt(MODEL_WIDTH)
    mixed = random_noise
    return jnp.clip(mixed, -1.0, 1.0).astype(jnp.bfloat16)


def draw_tokens(key, part):
    normal_part = jnp.clip(jax.random.normal(jax.random.fold_in(key, 3), (SEQUENCE_TOKENS, MODEL_WIDTH), jnp.float32), -6.0, 6.0)
    result = normal_part
    return result.astype(jnp.bfloat16)


def draw_span_order(key, part):
    shuffled = jax.random.permutation(jax.random.fold_in(key, 7), N_CTX).astype(jnp.int32)
    return jnp.stack([shuffled, 2 * N_CTX - 1 - shuffled], axis=1).astype(jnp.int32)


def block_levels(stream_key, extent, pieces, low, largest):
    factor_of, own = 1.0, jax.random.fold_in(stream_key, 6)
    for position, shards_of in pieces:
        draws = jnp.exp(jax.random.uniform(jax.random.fold_in(own, position), (shards_of,), jnp.float32, low / len(pieces), largest / len(pieces)))
        factor_of = factor_of * jnp.repeat(draws, extent[position] // shards_of).reshape([-1 if axis == position else 1 for axis in range(len(extent))])
    return factor_of


def bell_draw(stream_key, dims, spread, most, split=(), kind=jnp.bfloat16):
    factor_of = block_levels(stream_key, dims, split, -0.22, 0.18) if split else 1.0
    values = jax.random.normal(stream_key, dims, jnp.float32) * spread * factor_of
    return jnp.minimum(jnp.maximum(values, -most), most).astype(kind)


def setup_inputs(seed: int = 0) -> dict:
    arg_keys = jax.random.split(jax.random.key(seed), 7)
    return {
        "tokens": draw_tokens(jax.random.fold_in(arg_keys[6], 71), 0),
        "w_query": draw_w_query(jax.random.fold_in(arg_keys[6], 71), 0),
        "key_matrix": draw_key_matrix(jax.random.fold_in(arg_keys[6], 71), 0),
        "value_matrix": bell_draw(arg_keys[3], (MODEL_WIDTH, KEY_HEADS * HEAD_SIZE), MODEL_WIDTH ** -0.5, 0.078125, ((1, 4),)),
        "w_out": bell_draw(arg_keys[4], (QUERY_HEADS * HEAD_SIZE, MODEL_WIDTH), (QUERY_HEADS * HEAD_SIZE) ** -0.5, 0.109375, ((0, 4),)),
        "span_order": draw_span_order(jax.random.fold_in(arg_keys[6], 71), 0),
    }


ROPE_BASE = 1000000.0

def rotary_embed(values, token_positions):
    half = values.shape[-1] // 2
    freq = ROPE_BASE ** (-(jnp.arange(half, dtype=jnp.float32) * 2.0) / values.shape[-1])
    angle = token_positions[:, None] * freq[None, :]
    cosine = jnp.cos(angle)[:, None, :]
    sine = jnp.sin(angle)[:, None, :]
    first = values[..., :half]
    second = values[..., half:]
    return jnp.concatenate([first * cosine - second * sine, second * cosine + first * sine], axis=-1)

def reference(tokens, w_query, key_matrix, value_matrix, w_out, span_order):
    flat = span_order.reshape(-1).astype(jnp.int32)
    rows = jnp.arange(SEQUENCE_TOKENS, dtype=jnp.int32)
    token_positions = (flat[rows // SPAN_TOKENS] * SPAN_TOKENS + rows % SPAN_TOKENS).astype(jnp.float32)
    query_rows = rotary_embed(jnp.dot(tokens, w_query, preferred_element_type=jnp.float32).reshape(SEQUENCE_TOKENS, QUERY_HEADS, HEAD_SIZE), token_positions).astype(jnp.bfloat16)
    key = rotary_embed(jnp.dot(tokens, key_matrix, preferred_element_type=jnp.float32).reshape(SEQUENCE_TOKENS, KEY_HEADS, HEAD_SIZE), token_positions).astype(jnp.bfloat16)
    value_rows = jnp.dot(tokens, value_matrix, preferred_element_type=jnp.float32).astype(jnp.bfloat16).reshape(SEQUENCE_TOKENS, KEY_HEADS, HEAD_SIZE)
    query_grouped = query_rows.reshape(N_CTX, 2 * SPAN_TOKENS, KEY_HEADS, QUERY_PER_KEY, HEAD_SIZE).transpose(2, 1, 0, 3, 4)
    query_grouped = query_grouped.transpose(0, 2, 1, 3, 4)
    block_pos = token_positions.reshape(N_CTX, 2 * SPAN_TOKENS)
    keys_t = key.transpose(1, 0, 2)
    values_t = value_rows.transpose(1, 0, 2)
    inv_scale = 1.0 / math.sqrt(HEAD_SIZE)

    def per_head(args):
        query_g, key_g, value_g = args
        key_f = key_g.astype(jnp.float32)
        value_f = value_g.astype(jnp.float32)

        def per_block(inner):
            query_b, pos_b = inner
            score = jnp.einsum('qgd,kd->gqk', query_b.astype(jnp.float32), key_f) * inv_scale
            keep = token_positions[None, None, :] <= pos_b[None, :, None]
            score = jnp.where(keep, score, -1e+30)
            top = lax.optimization_barrier(jnp.max(score, axis=-1, keepdims=True))
            weight = jnp.where(keep, jnp.exp(score - top), 0.0)
            total = lax.optimization_barrier(jnp.sum(weight, axis=-1))
            weight_b = weight.astype(jnp.bfloat16).astype(jnp.float32)
            mixed = jnp.einsum('gqk,kd->gqd', weight_b, value_f) / total[..., None]
            return mixed.astype(jnp.bfloat16).transpose(1, 0, 2)
        return lax.map(per_block, (query_g, block_pos))
    heads = lax.map(per_head, (query_grouped, keys_t, values_t))
    heads_out = heads.transpose(1, 2, 0, 3, 4).reshape(SEQUENCE_TOKENS, QUERY_HEADS * HEAD_SIZE)
    per = QUERY_HEADS * HEAD_SIZE // N_TP
    attended = jnp.zeros((SEQUENCE_TOKENS, MODEL_WIDTH), jnp.float32)
    for group_index in range(N_TP):
        partial_value = jnp.dot(heads_out[:, group_index * per:(group_index + 1) * per], w_out[group_index * per:(group_index + 1) * per], preferred_element_type=jnp.float32).astype(jnp.bfloat16)
        partial_value = lax.optimization_barrier(partial_value)
        attended = attended + partial_value.astype(jnp.float32)
    return attended.astype(jnp.bfloat16)
```

```python
import functools
import math

import jax
import jax.numpy as jnp
from jax import lax
from jax.experimental import pallas as pl
from jax.experimental.pallas import tpu as pltpu
from jax.sharding import PartitionSpec as P

ROPE_BASE = 1000000.0
NEG = -1e30
SPAN = 256
HALF = 128
HEAD = 128
GROUP = 6
SETS = 32
QUAD = 4
QSCALE = math.log2(math.e) / math.sqrt(HEAD)

F32 = jnp.float32
BF16 = jnp.bfloat16

ANY = pl.BlockSpec(memory_space=pl.ANY)
SMEM = pl.BlockSpec(memory_space=pltpu.SMEM)
VMEM = pl.BlockSpec(memory_space=pltpu.VMEM)


def ctx_perm(dx, dz, dy):
    return [
        (
            x * 16 + z * 4 + y,
            ((x + dx) % 2) * 16 + ((z + dz) % 4) * 4 + (y + dy) % 4,
        )
        for x in range(2)
        for z in range(4)
        for y in range(4)
    ]


XS = ctx_perm(1, 0, 0)
YP, YM = ctx_perm(0, 0, 1), ctx_perm(0, 0, -1)
ZP, ZM = ctx_perm(0, 1, 0), ctx_perm(0, -1, 0)
CORE = [(0, 1), (1, 0), (2, 3), (3, 2)]
CHIP = [(0, 2), (2, 0), (1, 3), (3, 1)]


def project_kernel(t0, t1, wq, wk, wv, cos, sin, q_out, k_out, v_out, qa, ka, va):
    step = pl.program_id(0)

    @pl.when(step == 0)
    def _():
        qa[...] = jnp.zeros_like(qa)
        ka[...] = jnp.zeros_like(ka)
        va[...] = jnp.zeros_like(va)

    rows = jnp.concatenate([t0[...], t1[...]], axis=0)
    qa[...] += jnp.dot(rows, wq[...], preferred_element_type=F32)
    ka[...] += jnp.dot(rows, wk[...], preferred_element_type=F32)
    va[...] += jnp.dot(rows, wv[...], preferred_element_type=F32)

    @pl.when(step == pl.num_programs(0) - 1)
    def _():
        c, s = cos[...], sin[...]

        def rope(u):
            return u * c + pltpu.roll(u, HEAD // 2, axis=1) * s

        for h in range(GROUP):
            u = qa[:, h * HEAD : (h + 1) * HEAD]
            q_out[h] = (rope(u) * QSCALE).astype(BF16)
        k_out[...] = rope(ka[...]).astype(BF16)
        v_out[...] = va[...].astype(BF16)


def project(t0, t1, wq, wk, wv, cos, sin):
    width = wq.shape[0]
    chunk = 1024
    return pl.pallas_call(
        project_kernel,
        grid=(width // chunk,),
        in_specs=[
            pl.BlockSpec((HALF, chunk), lambda i: (0, i)),
            pl.BlockSpec((HALF, chunk), lambda i: (0, i)),
            pl.BlockSpec((chunk, GROUP * HEAD), lambda i: (i, 0)),
            pl.BlockSpec((chunk, HEAD), lambda i: (i, 0)),
            pl.BlockSpec((chunk, HEAD), lambda i: (i, 0)),
            pl.BlockSpec((SPAN, HEAD), lambda i: (0, 0)),
            pl.BlockSpec((SPAN, HEAD), lambda i: (0, 0)),
        ],
        out_specs=[
            pl.BlockSpec((GROUP, SPAN, HEAD), lambda i: (0, 0, 0)),
            pl.BlockSpec((SPAN, HEAD), lambda i: (0, 0)),
            pl.BlockSpec((SPAN, HEAD), lambda i: (0, 0)),
        ],
        out_shape=[
            jax.ShapeDtypeStruct((GROUP, SPAN, HEAD), BF16),
            jax.ShapeDtypeStruct((SPAN, HEAD), BF16),
            jax.ShapeDtypeStruct((SPAN, HEAD), BF16),
        ],
        scratch_shapes=[
            pltpu.VMEM((SPAN, GROUP * HEAD), F32),
            pltpu.VMEM((SPAN, HEAD), F32),
            pltpu.VMEM((SPAN, HEAD), F32),
        ],
        name="project",
    )(t0, t1, wq, wk, wv, cos, sin)


def attend_kernel(*refs, count, first, last):
    scal, slot = refs[:2]
    refs = list(refs[2:])
    q_ref = refs.pop(0)
    if not first:
        m_in, l_in, a_in = refs[:3]
        refs = refs[3:]
    k0, k1, k3, k2a, k2b, v0, v1, v3, v2a, v2b = refs[:10]
    refs = refs[10:]
    if last:
        o_ref = refs.pop(0)
        m, l, acc = refs[:3]
        refs = refs[3:]
    else:
        m, l, acc = refs[:3]
        refs = refs[3:]
    kv, vv, sems = refs
    copies = []

    def copy(src, dst):
        c = pltpu.make_async_copy(src, dst, sems.at[len(copies)])
        c.start()
        copies.append(c)

    copy(k0, kv.at[0])
    copy(k1, kv.at[1])
    copy(k3, kv.at[3])
    copy(k2a, kv.at[2, pl.ds(0, 2)])
    copy(k2b, kv.at[2, pl.ds(2, 2)])
    copy(v0, vv.at[:, 0])
    copy(v1, vv.at[:, 1])
    copy(v3, vv.at[:, 3])
    copy(v2a, vv.at[pl.ds(0, 2), 2])
    copy(v2b, vv.at[pl.ds(2, 2), 2])
    if first:
        m[...] = jnp.full(m.shape, NEG, F32)
        l[...] = jnp.zeros(l.shape, F32)
        acc[...] = jnp.zeros(acc.shape, F32)
    else:
        m[...] = m_in[...]
        l[...] = l_in[...]
        acc[...] = a_in[...]
    for c in copies:
        c.wait()
    base = scal[count]
    shift = scal[count + 1]

    def tile(ref, idx):
        return ref[idx // 8, (idx // 2) % 4, idx % 2]

    for n in range(count):
        rel = scal[n] - base

        def step(i, masked, n=n, rel=rel):
            idx = [slot[i * QUAD + j] for j in range(QUAD)]
            k = jnp.concatenate([tile(kv, j) for j in idx], axis=0)
            v = jnp.concatenate([tile(vv, j) for j in idx], axis=0)
            for h in range(GROUP):
                s = lax.dot_general(
                    q_ref[n, h], k, (((1,), (1,)), ((), ())), preferred_element_type=F32
                )
                if masked:
                    row = lax.broadcasted_iota(jnp.int32, s.shape, 0)
                    col = lax.broadcasted_iota(jnp.int32, s.shape, 1)
                    qp = rel * SPAN + ((row + shift) & (SPAN - 1))
                    kp = i * (QUAD * SPAN) + (col // SPAN) * SPAN
                    kp = kp + ((col + shift) & (SPAN - 1))
                    s = jnp.where(kp <= qp, s, NEG)
                m_old = m[n, h]
                m_new = jnp.maximum(m_old, jnp.max(s, axis=1, keepdims=True))
                alpha = jnp.exp2(m_old - m_new)
                p = jnp.exp2(s - jnp.concatenate([m_new] * (QUAD * 2), axis=1))
                m[n, h] = m_new
                part = p[:, :HEAD]
                for c in range(1, QUAD * 2):
                    part = part + p[:, c * HEAD : (c + 1) * HEAD]
                l[n, h] = alpha * l[n, h] + part
                acc[n, h] = alpha * acc[n, h] + jnp.dot(
                    p.astype(BF16), v, preferred_element_type=F32
                )

        full = jnp.clip(rel // QUAD, 0, SETS // QUAD)

        def loop(i, c, step=step):
            step(i, False)
            return c

        lax.fori_loop(0, full, loop, 0)

        @pl.when((rel >= 0) & (rel < SETS))
        def _(step=step, rel=rel):
            step(rel // QUAD, True)

        if last:
            for h in range(GROUP):
                total = jnp.sum(l[n, h], axis=1, keepdims=True)
                o_ref[n, :, h * HEAD : (h + 1) * HEAD] = (acc[n, h] / total).astype(BF16)


def attend(scal, slot, q, state, keys, values, last):
    count = q.shape[0]
    first = state is None
    shape = (count, GROUP, SPAN, HEAD)
    args = [scal, slot, q] + ([] if first else list(state)) + list(keys) + list(values)
    scratch = [
        pltpu.VMEM((4, 4, 2, SPAN, HEAD), BF16),
        pltpu.VMEM((4, 4, 2, SPAN, HEAD), BF16),
        pltpu.SemaphoreType.DMA((10,)),
    ]
    if last:
        out_shape = jax.ShapeDtypeStruct((count, SPAN, GROUP * HEAD), BF16)
        out_specs = VMEM
        scratch = [pltpu.VMEM(shape, F32)] * 3 + scratch
    else:
        out_shape = [jax.ShapeDtypeStruct(shape, F32)] * 3
        out_specs = [VMEM] * 3
    return pl.pallas_call(
        functools.partial(attend_kernel, count=count, first=first, last=last),
        in_specs=[SMEM, SMEM, VMEM] + ([] if first else [VMEM] * 3) + [ANY] * 10,
        out_specs=out_specs,
        out_shape=out_shape,
        scratch_shapes=scratch,
        compiler_params=pltpu.CompilerParams(vmem_limit_bytes=56 << 20),
        name="attend",
    )(*args)


def ring(block, plus, minus):
    three = lax.ppermute(block, "ctx", plus)
    one = lax.ppermute(block, "ctx", minus)
    half = block.shape[0] // 2
    two_a = lax.ppermute(three[:half], "ctx", plus)
    two_b = lax.ppermute(one[half:], "ctx", minus)
    return block, one, three, two_a, two_b


def gather_kv(k, v):
    both = jnp.stack([k, v])
    other = lax.ppermute(both, "ctx", XS)
    keys = jnp.stack([k, other[0]])
    values = jnp.stack([v, other[1]])

    def line(block, plus, minus):
        own, one, three, two_a, two_b = ring(block, plus, minus)
        return jnp.stack([own, one, jnp.concatenate([two_a, two_b]), three])

    keys = line(keys, YP, YM)
    values = line(values, ZP, ZM)
    return ring(keys, ZP, ZM), ring(values, YP, YM)


def slots(order, base, rank):
    r = jnp.arange(SETS, dtype=jnp.int32)
    dx = (r // 16 - rank // 16) % 2
    dz = ((r // 4) % 4 - (rank // 4) % 4) % 4
    dy = (r % 4 - rank % 4) % 4
    place = dz * 8 + dy * 2 + dx
    hit = (order - base)[None, :] == jnp.arange(SETS, dtype=jnp.int32)[:, None]
    return jnp.sum(jnp.where(hit, place[None, :], 0), axis=1).astype(jnp.int32)


def rope_tables(span_id, shift):
    half = HEAD // 2
    freq = ROPE_BASE ** (-(jnp.arange(half, dtype=F32) * 2.0) / HEAD)
    row = (jnp.arange(SPAN, dtype=jnp.int32) + shift) % SPAN
    pos = (span_id * SPAN + row).astype(F32)
    angle = pos[:, None] * freq[None, :]
    c, s = jnp.cos(angle), jnp.sin(angle)
    return jnp.concatenate([c, c], axis=1), jnp.concatenate([-s, s], axis=1)


def body(tokens, w_query, key_matrix, value_matrix, w_out, span_order):
    rank = lax.axis_index("ctx")
    tp = lax.axis_index("tp")
    chip, core = tp // 2, tp % 2
    shift = core * HALF
    order = span_order.astype(jnp.int32)
    mine = lax.dynamic_slice(order, (rank, jnp.int32(0)), (1, 2)).reshape(2)
    near_order = jnp.where(chip == 0, order[:, 0], order[:, 1])
    far_order = jnp.where(chip == 0, order[:, 1], order[:, 0])
    near_span = jnp.where(chip == 0, mine[0], mine[1])
    far_span = jnp.where(chip == 0, mine[1], mine[0])
    near_base = chip * SETS
    far_base = SETS - near_base
    near_slot = slots(near_order, near_base, rank)
    far_slot = slots(far_order, far_base, rank)

    far_own = lax.ppermute(tokens, "tp", CHIP)
    sibling = lax.ppermute(tokens, "tp", CORE)
    weights = (w_query, key_matrix, value_matrix)
    q_near, k_near, v_near = project(tokens, sibling, *weights, *rope_tables(near_span, shift))
    near_keys, near_values = gather_kv(k_near, v_near)

    far_sibling = lax.ppermute(far_own, "tp", CORE)
    q_far, k_far, v_far = project(far_own, far_sibling, *weights, *rope_tables(far_span, shift))
    far_keys, far_values = gather_kv(k_far, v_far)

    def scalars(*spans_base):
        return jnp.stack([*spans_base, shift]).astype(jnp.int32)

    state = attend(
        scalars(far_span, near_span, near_base),
        near_slot,
        jnp.stack([q_far, q_near]),
        None,
        near_keys,
        near_values,
        False,
    )
    heads_far = attend(
        scalars(far_span, far_base),
        far_slot,
        q_far[None],
        [t[:1] for t in state],
        far_keys,
        far_values,
        True,
    )
    heads_near = attend(
        scalars(near_span, far_base),
        far_slot,
        q_near[None],
        [t[1:] for t in state],
        far_keys,
        far_values,
        True,
    )

    def pair_sum(heads):
        partial = jnp.dot(heads[0], w_out, preferred_element_type=F32).astype(BF16)
        got = lax.ppermute(partial[HALF:], "tp", CORE)
        return partial[:HALF].astype(F32) + got.astype(F32)

    far_sum = pair_sum(heads_far).astype(BF16)
    got = lax.ppermute(far_sum, "tp", CHIP)
    near_sum = pair_sum(heads_near)
    return (near_sum + got.astype(F32)).astype(BF16)


def solution(mesh):
    return jax.shard_map(
        body,
        mesh=mesh,
        in_specs=(
            P(("ctx", "tp"), None),
            P(None, "tp"),
            P(None, "tp"),
            P(None, "tp"),
            P("tp", None),
            P(),
        ),
        out_specs=P(("ctx", "tp"), None),
        check_vma=False,
    )
```

```python
import functools
import math

import jax
import jax.numpy as jnp
from jax import lax
from jax.experimental import pallas as pl
from jax.experimental.pallas import tpu as pltpu
from jax.sharding import PartitionSpec as P

ROPE_BASE = 1000000.0
NEG = -1e30
SPAN = 256
HALF = 128
HEAD = 128
GROUP = 6
SETS = 32
QUAD = 4
PIECES = 2
QSCALE = math.log2(math.e) / math.sqrt(HEAD)

F32 = jnp.float32
BF16 = jnp.bfloat16

ANY = pl.BlockSpec(memory_space=pl.ANY)
SMEM = pl.BlockSpec(memory_space=pltpu.SMEM)
VMEM = pl.BlockSpec(memory_space=pltpu.VMEM)


def ctx_perm(dx, dz, dy):
    return [
        (
            x * 16 + z * 4 + y,
            ((x + dx) % 2) * 16 + ((z + dz) % 4) * 4 + (y + dy) % 4,
        )
        for x in range(2)
        for z in range(4)
        for y in range(4)
    ]


XS = ctx_perm(1, 0, 0)
YP, YM = ctx_perm(0, 0, 1), ctx_perm(0, 0, -1)
ZP, ZM = ctx_perm(0, 1, 0), ctx_perm(0, -1, 0)
Y2, Z2 = ctx_perm(0, 0, 2), ctx_perm(0, 2, 0)
CORE = [(0, 1), (1, 0), (2, 3), (3, 2)]
CHIP = [(0, 2), (2, 0), (1, 3), (3, 1)]


CHUNK = 2048


def rope(u, c, s):
    return u * c + pltpu.roll(u, HEAD // 2, axis=1) * s


def accumulate(rows, w, acc):
    step = pl.program_id(0)
    product = jnp.dot(rows, w[...], preferred_element_type=F32)

    @pl.when(step == 0)
    def _():
        acc[...] = product

    @pl.when(step > 0)
    def _():
        acc[...] += product


def kv_kernel(*refs):
    wk, wv, cos, sin, out, ka, va = refs[-7:]
    rows = jnp.concatenate([t[...] for t in refs[:-7]], axis=0)
    accumulate(rows, wk, ka)
    accumulate(rows, wv, va)

    @pl.when(pl.program_id(0) == pl.num_programs(0) - 1)
    def _():
        out[0] = rope(ka[...], cos[...], sin[...]).astype(BF16)
        out[1] = va[...].astype(BF16)


def q_kernel(*refs):
    wq, cos, sin, out, qa = refs[-5:]
    rows = jnp.concatenate([t[...] for t in refs[:-5]], axis=0)
    accumulate(rows, wq, qa)

    @pl.when(pl.program_id(0) == pl.num_programs(0) - 1)
    def _():
        for h in range(GROUP):
            u = rope(qa[:, h * HEAD : (h + 1) * HEAD], cos[...], sin[...])
            out[h] = (u * QSCALE).astype(BF16)


def project(kernel, rows, weights, tables, blocks, name):
    def fixed(shape):
        return pl.BlockSpec(shape, lambda i: (0,) * len(shape))

    return pl.pallas_call(
        kernel,
        grid=(rows[0].shape[1] // CHUNK,),
        in_specs=[pl.BlockSpec((t.shape[0], CHUNK), lambda i: (0, i)) for t in rows]
        + [pl.BlockSpec((CHUNK, w.shape[1]), lambda i: (i, 0)) for w in weights]
        + [fixed((SPAN, HEAD))] * 2,
        out_specs=fixed((blocks, SPAN, HEAD)),
        out_shape=jax.ShapeDtypeStruct((blocks, SPAN, HEAD), BF16),
        scratch_shapes=[pltpu.VMEM((SPAN, w.shape[1]), F32) for w in weights],
        compiler_params=pltpu.CompilerParams(vmem_limit_bytes=40 << 20),
        name=name,
    )(*rows, *weights, *tables)


def out_kernel(heads, w, keep, send):
    both = jnp.dot(heads[...], w[...], preferred_element_type=F32).astype(BF16)
    keep[...] = both[:HALF]
    send[...] = both[HALF:]


def project_out(heads, w, first, width):
    block = 1536
    start = first // block
    return pl.pallas_call(
        out_kernel,
        grid=(width // block,),
        in_specs=[
            pl.BlockSpec(heads.shape, lambda i: (0, 0)),
            pl.BlockSpec((w.shape[0], block), lambda i: (0, i + start)),
        ],
        out_specs=[pl.BlockSpec((HALF, block), lambda i: (0, i))] * 2,
        out_shape=[jax.ShapeDtypeStruct((HALF, width), BF16)] * 2,
        name="project_out",
    )(heads, w)


def attend_kernel(*refs, n_q, n_sets, resume, limits, last):
    scal, slot = refs[:2]
    refs = list(refs[2:])
    qs = [refs.pop(0) for _ in range(n_q)]
    state_in = None if resume is None else refs.pop(0)
    sets = [[refs.pop(0) for _ in range(10)] for _ in range(n_sets)]
    out, q, st, kv, vv, sems = refs
    rel, shift, chip = scal[0], scal[1], scal[2]

    def fetch(q_src, source):
        k0, k1, k2a, k2b, k3, v0, v1, v2a, v2b, v3 = source
        copies = [
            pltpu.make_async_copy(src, dst, sems.at[i])
            for i, (src, dst) in enumerate(
                [
                    (q_src, q),
                    (k0, kv.at[0]),
                    (k1, kv.at[1]),
                    (k2a, kv.at[2, pl.ds(0, 2)]),
                    (k2b, kv.at[2, pl.ds(2, 2)]),
                    (k3, kv.at[3]),
                    (v0, vv.at[:, 0]),
                    (v1, vv.at[:, 1]),
                    (v2a, vv.at[pl.ds(0, 2), 2]),
                    (v2b, vv.at[pl.ds(2, 2), 2]),
                    (v3, vv.at[:, 3]),
                ]
            )
        ]
        for c in copies:
            c.start()
        for c in copies:
            c.wait()

    def fresh():
        st[0] = jnp.full(st.shape[1:], NEG, F32)
        st[1] = jnp.zeros(st.shape[1:], F32)
        st[2] = jnp.zeros(st.shape[1:], F32)

    def resumed():
        c = pltpu.make_async_copy(state_in, st, sems.at[11])
        c.start()
        c.wait()

    for place in range(2):

        @pl.when(chip == place)
        def _(place=place):
            fetch(qs[place % n_q], sets[place % n_sets])
            if resume == "all" or resume == place:
                resumed()
            else:
                fresh()

    full = jnp.clip(rel // QUAD, 0, SETS // QUAD)
    total = full + ((rel >= 0) & (rel < SETS)).astype(jnp.int32)

    def tile(ref, idx):
        return ref[idx // 8, (idx // 2) % 4, idx % 2]

    def head(h, i, k, v, masked):
        s = lax.dot_general(q[h], k, (((1,), (1,)), ((), ())), preferred_element_type=F32)
        if masked:
            row = lax.broadcasted_iota(jnp.int32, s.shape, 0)
            col = lax.broadcasted_iota(jnp.int32, s.shape, 1)
            qp = rel * SPAN + ((row + shift) & (SPAN - 1))
            kp = i * (QUAD * SPAN) + (col // SPAN) * SPAN
            kp = kp + ((col + shift) & (SPAN - 1))
            s = jnp.where(kp <= qp, s, NEG)
        m_old = st[0, h]
        m_new = jnp.maximum(m_old, jnp.max(s, axis=1, keepdims=True))
        alpha = jnp.exp2(m_old - m_new)
        p = jnp.exp2(s - jnp.concatenate([m_new] * (QUAD * 2), axis=1))
        st[0, h] = m_new
        part = p[:, :HEAD]
        for c in range(1, QUAD * 2):
            part = part + p[:, c * HEAD : (c + 1) * HEAD]
        st[1, h] = alpha * st[1, h] + part
        st[2, h] = alpha * st[2, h] + jnp.dot(p.astype(BF16), v, preferred_element_type=F32)

    def loop(i, c):
        idx = [slot[i * QUAD + j] for j in range(QUAD)]

        def operands():
            return (
                jnp.concatenate([tile(kv, j) for j in idx], axis=0),
                jnp.concatenate([tile(vv, j) for j in idx], axis=0),
            )

        @pl.when(i < full)
        def _():
            k, v = operands()
            for h in range(GROUP):
                head(h, i, k, v, False)

        @pl.when(i >= full)
        def _():
            def one(h, c):
                head(h, i, *operands(), True)
                return c

            lax.fori_loop(0, GROUP, one, 0)

        return c

    low, high = limits
    lax.fori_loop(
        jnp.minimum(low, total), total if high is None else jnp.minimum(high, total), loop, 0
    )
    if last:
        for h in range(GROUP):
            whole = jnp.sum(st[1, h], axis=1, keepdims=True)
            out[:, h * HEAD : (h + 1) * HEAD] = (st[2, h] / whole).astype(BF16)
    else:
        c = pltpu.make_async_copy(st, out, sems.at[11])
        c.start()
        c.wait()


def attend(scal, slot, qs, state, sets, resume=None, limits=(0, None), last=False):
    shape = (3, GROUP, SPAN, HEAD)
    args = [scal, slot, *qs] + ([] if resume is None else [state])
    for keys, values in sets:
        args += [*keys, *values]
    return pl.pallas_call(
        functools.partial(
            attend_kernel,
            n_q=len(qs),
            n_sets=len(sets),
            resume=resume,
            limits=limits,
            last=last,
        ),
        in_specs=[SMEM, SMEM] + [ANY] * (len(args) - 2),
        out_specs=VMEM if last else ANY,
        out_shape=jax.ShapeDtypeStruct((SPAN, GROUP * HEAD), BF16)
        if last
        else jax.ShapeDtypeStruct(shape, F32),
        scratch_shapes=[
            pltpu.VMEM((GROUP, SPAN, HEAD), BF16),
            pltpu.VMEM(shape, F32),
            pltpu.VMEM((4, 4, 2, SPAN, HEAD), BF16),
            pltpu.VMEM((4, 4, 2, SPAN, HEAD), BF16),
            pltpu.SemaphoreType.DMA((12,)),
        ],
        compiler_params=pltpu.CompilerParams(vmem_limit_bytes=56 << 20),
        name="attend",
    )(*args)


def after(values, *tokens):
    return lax.optimization_barrier((values, *tokens))[0]


def short_ring(block, plus, minus, two):
    return jnp.stack(
        [
            block,
            lax.ppermute(block, "ctx", minus),
            lax.ppermute(block, "ctx", two),
            lax.ppermute(block, "ctx", plus),
        ]
    )


def spread(kv, *tokens):
    other = after(lax.ppermute(kv, "ctx", XS), *tokens)
    keys = jnp.stack([kv[0], other[0]])
    values = jnp.stack([kv[1], other[1]])
    return short_ring(keys, YP, YM, Y2), short_ring(values, ZP, ZM, Z2)


def first_hop(keys, values):
    return [
        (
            block,
            lax.ppermute(block, "ctx", plus),
            lax.ppermute(block, "ctx", minus),
        )
        for block, plus, minus in ((keys, ZP, ZM), (values, YP, YM))
    ]


def second_hop(hops):
    done = []
    for (own, three, one), (plus, minus) in zip(hops, ((ZP, ZM), (YP, YM))):
        two_a = lax.ppermute(three[:2], "ctx", plus)
        two_b = lax.ppermute(one[2:], "ctx", minus)
        done.append((own, one, two_a, two_b, three))
    return done


def slots(order, base, rank):
    r = jnp.arange(SETS, dtype=jnp.int32)
    dx = (r // 16 - rank // 16) % 2
    dz = ((r // 4) % 4 - (rank // 4) % 4) % 4
    dy = (r % 4 - rank % 4) % 4
    place = dz * 8 + dy * 2 + dx
    hit = (order - base)[None, :] == jnp.arange(SETS, dtype=jnp.int32)[:, None]
    return jnp.sum(jnp.where(hit, place[None, :], 0), axis=1).astype(jnp.int32)


def rope_tables(span_id, shift):
    half = HEAD // 2
    freq = ROPE_BASE ** (-(jnp.arange(half, dtype=F32) * 2.0) / HEAD)
    row = (jnp.arange(SPAN, dtype=jnp.int32) + shift) % SPAN
    pos = (span_id * SPAN + row).astype(F32)
    angle = pos[:, None] * freq[None, :]
    c, s = jnp.cos(angle), jnp.sin(angle)
    return jnp.concatenate([c, c], axis=1), jnp.concatenate([-s, s], axis=1)


def body(tokens, w_query, key_matrix, value_matrix, w_out, span_order):
    rank = lax.axis_index("ctx")
    tp = lax.axis_index("tp")
    chip, core = tp // 2, tp % 2
    shift = core * HALF
    order = span_order.astype(jnp.int32)
    mine = lax.dynamic_slice(order, (rank, jnp.int32(0)), (1, 2)).reshape(2)
    near_order = jnp.where(chip == 0, order[:, 0], order[:, 1])
    far_order = jnp.where(chip == 0, order[:, 1], order[:, 0])
    near_span = jnp.where(chip == 0, mine[0], mine[1])
    far_span = jnp.where(chip == 0, mine[1], mine[0])
    near_base = chip * SETS
    far_base = SETS - near_base
    near_slot = slots(near_order, near_base, rank)
    far_slot = slots(far_order, far_base, rank)

    kv_weights = (key_matrix, value_matrix)

    def kv_of(rows, tables):
        return project(kv_kernel, rows, kv_weights, tables, 2, "project_kv")

    def q_of(rows, tables):
        return project(q_kernel, rows, (w_query,), tables, GROUP, "project_q")

    rows = tokens.shape[0] // 2
    far_a = lax.ppermute(tokens[:rows], "tp", CHIP)
    sibling = lax.ppermute(tokens, "tp", CORE)
    near_tables = rope_tables(near_span, shift)
    far_tables = rope_tables(far_span, shift)
    kv_near = kv_of([tokens, sibling], near_tables)
    q_near = q_of([tokens, after(sibling, kv_near)], near_tables)
    far_b = lax.ppermute(after(tokens[rows:], q_near), "tp", CHIP)
    far_sa = lax.ppermute(far_a, "tp", CORE)
    near8 = spread(kv_near, q_near)
    near_hop = first_hop(*near8)
    far_b = after(far_b, near8)
    far_sb = lax.ppermute(far_b, "tp", CORE)
    near_kv = second_hop(near_hop)

    kv_far = kv_of([far_a, far_b, far_sa, far_sb], far_tables)
    q_far = q_of([far_a, far_b, far_sa, after(far_sb, kv_far)], far_tables)
    far8 = spread(kv_far, q_far)
    far_hop = first_hop(*far8)

    def scalars(rel):
        return jnp.stack([rel, shift, chip]).astype(jnp.int32)

    near_kv = [t for half in near_kv for t in half]
    near_set = (near_kv[:5], near_kv[5:])
    early = scalars(jnp.where(chip == 0, far_span, near_span) - near_base)
    early_q = [q_far, q_near]
    state = attend(after(early, far8), near_slot, early_q, None, [near_set], limits=(0, 4))
    far_hop = after(far_hop, state)
    far_set = second_hop(far_hop)
    state = attend(
        after(early, far_hop), near_slot, early_q, state, [near_set], "all", limits=(4, None)
    )
    heads_far = attend(
        scalars(far_span - far_base), far_slot, [q_far], state, [far_set], 0, last=True
    )
    width = w_out.shape[1]
    piece = width // PIECES

    def pair_sum(heads, i):
        keep, send = project_out(heads, w_out, i * piece, piece)
        got = lax.ppermute(send, "tp", CORE)
        return keep.astype(F32) + got.astype(F32)

    far_sums = [pair_sum(heads_far, i).astype(BF16) for i in range(PIECES)]
    crossed = [lax.ppermute(t, "tp", CHIP) for t in far_sums]
    heads_near = attend(
        after(scalars(near_span), far_sums),
        jnp.where(chip == 0, near_slot, far_slot),
        [q_near],
        state,
        [near_set, far_set],
        1,
        last=True,
    )
    return jnp.concatenate(
        [
            (pair_sum(heads_near, i) + crossed[i].astype(F32)).astype(BF16)
            for i in range(PIECES)
        ],
        axis=1,
    )


def solution(mesh):
    return jax.shard_map(
        body,
        mesh=mesh,
        in_specs=(
            P(("ctx", "tp"), None),
            P(None, "tp"),
            P(None, "tp"),
            P(None, "tp"),
            P("tp", None),
            P(),
        ),
        out_specs=P(("ctx", "tp"), None),
        check_vma=False,
    )
```
